32 devices in a mesh: half: 2 (over y), row: 4 (over z), col: 4 (over x, core).
Axes of the slice: x: 2, y: 2, z: 4, core: 2. Of those that a mesh axis runs over, the one named last changes fastest.
Arguments:
- children: bfloat16 [2, 512, 512, 512], P('half', 'row', 'col'), may hold values from -0.01171875 to 0.01171875
- operators: bfloat16 [2, 2, 4, 512, 512], P('half'), may hold values from -1 to 1
- term_site: int32 [2, 5, 2], P('half'), may hold values from 0 to 3
- term_leg: int32 [2, 5], P('half'), may hold values from 0 to 2
- parent: bfloat16 [512, 512, 512], P(('half', 'row', 'col')), may hold values from -6 to 6
Outputs:
- updated: bfloat16 [512, 512, 512], P(('half', 'row', 'col'))
The draws below stay inside these ranges and needn't reach their ends.
Inputs may be any that keep to these rules, and one draw needn't show every extreme that they name: `term_site`: a site index into the child's operator table of 4 entries. `term_leg`: 0: the term acts on the first leg only, 1: on the second leg only, 2: on both.
All inputs are finite; a program needn't handle non-finite values.
Results may differ from the reference program's by a relative error of at most 0.0064.
Values may be sent and summed in bfloat16 or wider, within the bound.
A program may use at most 320 MiB of HBM per device.

```python
import jax
import jax.numpy as jnp
from jax import lax

B = 512
C = 512
TERMS = 5
SITES = 4


def touch_ends(entries, stream_key, least, high):
    longest = entries.shape.index(max(entries.shape))
    spots = []
    for shift in (0, 1):
        where = [jax.random.randint(jax.random.fold_in(stream_key, axis), (), 0, length) for axis, length in enumerate(entries.shape)]
        where[longest] = (where[longest] + shift) % entries.shape[longest]
        spots.append(tuple(where))
    return entries.at[spots[0]].set(least).at[spots[1]].set(high)


def block_levels(own_key, dims, cuts, least, top_value):
    gain = 1.0
    for dim, parts in cuts:
        draws = jax.random.uniform(jax.random.fold_in(jax.random.fold_in(own_key, 6), dim), (parts,), jnp.float32, least / len(cuts), top_value / len(cuts))
        gain = gain * jnp.repeat(jnp.exp(draws), dims[dim] // parts).reshape((-1,) + (1,) * (len(dims) - 1 - dim))
    return gain


def scatter_about(rng, shape, deviation, most, cuts=(), kind=jnp.bfloat16):
    array = jax.random.normal(rng, shape, jnp.float32) * deviation
    if len(cuts) > 0:
        array = block_levels(rng, shape, cuts, -0.22, 0.18) * array
    return jnp.clip(array, min=-most, max=most).astype(kind)


def setup_inputs(seed: int = 0) -> dict:
    splits = jax.random.split(jax.random.key(seed), 6)
    return {
        "children": scatter_about(splits[0], (2, B, B, B), (B * B) ** -0.5, 0.01171875, ((0, 2), (1, 4), (2, 4))),
        "operators": scatter_about(splits[1], (2, 2, SITES, B, B), (B // 16) ** -0.5, 1.0, ((0, 2),)),
        "term_site": touch_ends(jax.random.randint(splits[2], (2, TERMS, 2), 0, SITES), jax.random.fold_in(splits[2], 1), 0, SITES - 1).astype(jnp.int32),
        "term_leg": touch_ends(jax.random.randint(splits[3], (2, TERMS), 0, 3), jax.random.fold_in(splits[3], 1), 0, 2).astype(jnp.int32),
        "parent": scatter_about(splits[4], (C, B, B), 1.0, 6.0, ((0, 32),)),
    }


def apply_terms(block, table, site_ids, leg_codes):
    identity = jnp.eye(B, dtype=block.dtype)
    accumulated = jnp.zeros(block.shape, jnp.float32)
    for term in range(TERMS):
        left_op = jnp.where(leg_codes[term] != 1, table[0, site_ids[term, 0]], identity)
        right_op = jnp.where(leg_codes[term] != 0, table[1, site_ids[term, 1]], identity)
        inner = jnp.einsum('aik,jk->aij', block.astype(jnp.float32), right_op.astype(jnp.float32)).astype(jnp.bfloat16)
        accumulated = accumulated + jnp.einsum('ik,akj->aij', left_op.astype(jnp.float32), inner.astype(jnp.float32))
    return accumulated.astype(jnp.bfloat16)


def environment_of(child, table, site_ids, leg_codes):
    group = min(64, B)
    blocks = child.reshape(B // group, group, B, B)
    summed = lax.map(lambda piece: apply_terms(piece, table, site_ids, leg_codes), blocks)
    flat_child = child.reshape(B, B * B)
    flat_summed = summed.reshape(B, B * B)
    product = lax.dot_general(flat_child, flat_summed, (((1,), (1,)), ((), ())), preferred_element_type=jnp.float32)
    return product.astype(jnp.bfloat16)


def reference(children, operators, term_site, term_leg, parent):
    left_env = environment_of(children[0], operators[0], term_site[0], term_leg[0])
    right_env = environment_of(children[1], operators[1], term_site[1], term_leg[1])
    parent_wide = parent.astype(jnp.float32)
    first = jnp.einsum('ak,ckb->cab', left_env.astype(jnp.float32), parent_wide)
    second = jnp.einsum('bk,cak->cab', right_env.astype(jnp.float32), parent_wide)
    return (first + second).astype(jnp.bfloat16)
```

```python
import functools

import jax
import jax.numpy as jnp
from jax import lax
from jax.experimental import pallas as pl
from jax.experimental.pallas import tpu as pltpu
from jax.sharding import PartitionSpec as P


def terms_kernel(pieces, batch, groups, flags_ref, *refs):
    piece_refs = refs[:pieces]
    left_ref, right_ref = refs[pieces], refs[pieces + 1]
    out_refs = refs[pieces + 2 : 2 * pieces + 2]
    acc_ref = refs[-1]
    rows = piece_refs[0].shape[1]
    for item in range(batch):
        acc_ref[...] = jnp.zeros_like(acc_ref)

        @pl.when(flags_ref[groups] > 0)
        def _():
            block = jnp.concatenate([ref[item] for ref in piece_refs], axis=0)
            acc_ref[...] = jnp.dot(block, right_ref[groups], preferred_element_type=jnp.float32)

        for group in range(groups):

            @pl.when(flags_ref[group] > 0)
            def _():
                block = jnp.concatenate([ref[item] for ref in piece_refs], axis=0)
                inner = jnp.dot(block, right_ref[group], preferred_element_type=jnp.float32)
                acc_ref[...] += jnp.dot(
                    left_ref[group], inner.astype(jnp.bfloat16), preferred_element_type=jnp.float32
                )

        for place in range(pieces):
            out_refs[place][item] = acc_ref[place * rows : (place + 1) * rows, :].astype(jnp.bfloat16)


def apply_terms(flags, blocks, left_ops, right_ops):
    pieces = len(blocks)
    count, rows, bond = blocks[0].shape
    groups = left_ops.shape[0]
    batch = 2 if count % 2 == 0 else 1
    piece_spec = pl.BlockSpec((batch, rows, bond), lambda a, f: (a, 0, 0))
    flops = 2 * (2 * groups + 1) * count * bond**3
    moved = 4 * count * bond * bond
    return pl.pallas_call(
        functools.partial(terms_kernel, pieces, batch, groups),
        out_shape=[jax.ShapeDtypeStruct((count, rows, bond), jnp.bfloat16)] * pieces,
        grid_spec=pltpu.PrefetchScalarGridSpec(
            num_scalar_prefetch=1,
            grid=(count // batch,),
            in_specs=[piece_spec] * pieces
            + [
                pl.BlockSpec(left_ops.shape, lambda a, f: (0, 0, 0)),
                pl.BlockSpec(right_ops.shape, lambda a, f: (0, 0, 0)),
            ],
            out_specs=[piece_spec] * pieces,
            scratch_shapes=[pltpu.VMEM((bond, bond), jnp.float32)],
        ),
        compiler_params=pltpu.CompilerParams(dimension_semantics=("arbitrary",)),
        cost_estimate=pl.CostEstimate(flops=flops, bytes_accessed=moved, transcendentals=0),
        name="apply_terms",
    )(flags, *blocks, left_ops, right_ops)


MESH_ID = pl.DeviceIdType.MESH


def share_kernel(halves, rows, cols, parts_ref, out_ref, landed, send_sem, recv_sem, line_send, line_recv, plane_send, plane_recv):
    half, row, col = lax.axis_index("half"), lax.axis_index("row"), lax.axis_index("col")

    def place(dh, dr, dc):
        return {
            "half": lax.rem(half + dh, halves),
            "row": lax.rem(row + dr, rows),
            "col": lax.rem(col + dc, cols),
        }

    group = [(dr, dc) for dr in range(rows) for dc in range(cols) if (dr, dc) != (0, 0)]
    plane = [(dh, dc) for dh in range(halves) for dc in range(cols) if (dh, dc) != (0, 0)]
    barrier = pltpu.get_barrier_semaphore()
    greeted = [(0, dr, dc) for dr, dc in group] + [(dh, 0, dc) for dh, dc in plane if dh != 0]
    for spot in greeted:
        pl.semaphore_signal(barrier, inc=1, device_id=place(*spot), device_id_type=MESH_ID)
    pl.semaphore_wait(barrier, len(greeted))

    copies = []
    for dr, dc in group:
        spot = place(0, dr, dc)
        slot = dr * cols + dc
        copy = pltpu.make_async_remote_copy(
            src_ref=parts_ref.at[spot["col"] * rows + spot["row"]],
            dst_ref=landed.at[slot],
            send_sem=send_sem.at[slot],
            recv_sem=recv_sem.at[slot],
            device_id=spot,
            device_id_type=MESH_ID,
        )
        copy.start()
        copies.append(copy)
    total = parts_ref[col * rows + row].astype(jnp.float32)
    for (dr, dc), copy in zip(group, copies):
        copy.wait_recv()
        total = total + landed[dr * cols + dc].astype(jnp.float32)
    mine = (half * cols + col) * rows + row
    out_ref[mine] = total.astype(out_ref.dtype)

    line = []
    for dr in range(1, rows):
        copy = pltpu.make_async_remote_copy(
            src_ref=out_ref.at[mine],
            dst_ref=out_ref.at[mine],
            send_sem=line_send.at[dr],
            recv_sem=line_recv.at[dr],
            device_id=place(0, dr, 0),
            device_id_type=MESH_ID,
        )
        copy.start()
        line.append(copy)
    for copy in line:
        copy.wait_recv()
    block = pl.ds((half * cols + col) * rows, rows)
    for dh, dc in plane:
        slot = dh * cols + dc
        copy = pltpu.make_async_remote_copy(
            src_ref=out_ref.at[block],
            dst_ref=out_ref.at[block],
            send_sem=plane_send.at[slot],
            recv_sem=plane_recv.at[slot],
            device_id=place(dh, 0, dc),
            device_id_type=MESH_ID,
        )
        copy.start()
        copies.append(copy)
    for copy in copies[len(group) :]:
        copy.wait_recv()
    for copy in copies + line:
        copy.wait_send()


def share_environments(halves, rows, cols, partial):
    bond = partial.shape[0]
    slab = bond // (rows * cols)
    dma = pltpu.SemaphoreType.DMA
    return pl.pallas_call(
        functools.partial(share_kernel, halves, rows, cols),
        out_shape=jax.ShapeDtypeStruct((halves * cols * rows, slab, bond), jnp.bfloat16),
        in_specs=[pl.BlockSpec(memory_space=pltpu.VMEM)],
        out_specs=pl.BlockSpec(memory_space=pltpu.VMEM),
        scratch_shapes=[
            pltpu.VMEM((rows * cols, slab, bond), jnp.bfloat16),
            dma((rows * cols,)),
            dma((rows * cols,)),
            dma((rows,)),
            dma((rows,)),
            dma((halves * cols,)),
            dma((halves * cols,)),
        ],
        compiler_params=pltpu.CompilerParams(collective_id=0, has_side_effects=True),
        name="share_environments",
    )(partial.astype(jnp.bfloat16).reshape(rows * cols, slab, bond)).reshape(halves * bond, bond)


def parent_kernel(envs_ref, parent_ref, out_ref):
    bond = parent_ref.shape[1]
    plane = parent_ref[0]
    first = jnp.dot(envs_ref[:bond], plane, preferred_element_type=jnp.float32)
    second = lax.dot_general(
        plane, envs_ref[bond:], (((1,), (1,)), ((), ())), preferred_element_type=jnp.float32
    )
    out_ref[0] = (first + second).astype(out_ref.dtype)


def apply_to_parent(envs, parent):
    count, bond, _ = parent.shape
    spec = pl.BlockSpec((1, bond, bond), lambda c: (c, 0, 0))
    return pl.pallas_call(
        parent_kernel,
        out_shape=jax.ShapeDtypeStruct(parent.shape, parent.dtype),
        grid=(count,),
        in_specs=[pl.BlockSpec(envs.shape, lambda c: (0, 0)), spec],
        out_specs=spec,
        compiler_params=pltpu.CompilerParams(dimension_semantics=("arbitrary",)),
        cost_estimate=pl.CostEstimate(
            flops=4 * count * bond**3, bytes_accessed=4 * count * bond**2, transcendentals=0
        ),
        name="apply_to_parent",
    )(envs, parent)


def on_device(halves, rows, cols, children, operators, term_site, term_leg, parent):
    child = children[0]
    tops, firsts, bond = child.shape
    row = lax.axis_index("row")
    col = lax.axis_index("col")
    row_order = jnp.arange(rows) ^ row
    col_order = jnp.arange(cols) ^ col
    mine = tops // cols
    share = firsts // rows
    chunks = 4 if mine % 4 == 0 else 1
    step = mine // chunks

    def swap(value, axis, size, offset):
        if offset == 0:
            return value
        return lax.ppermute(value, axis, [(k, k ^ offset) for k in range(size)])

    table = operators[0].astype(jnp.float32)
    site_ids, leg_codes = term_site[0], term_leg[0]
    sites = table.shape[1]
    left_group = jnp.where(leg_codes != 1, site_ids[:, 0], sites)
    right_pick = jnp.where(leg_codes != 0, site_ids[:, 1], sites)
    in_group = (left_group[None, :] == jnp.arange(sites + 1)[:, None]).astype(jnp.float32)
    of_right = (right_pick[:, None] == jnp.arange(sites + 1)[None, :]).astype(jnp.float32)
    counts = jnp.sum(in_group[:, :, None] * of_right[None, :, :], axis=1)
    flags = (jnp.sum(counts, axis=1) > 0).astype(jnp.int32)
    turned = jnp.swapaxes(table[1], 1, 2)
    weights = counts[:, :sites, None, None] * turned[None]
    right_ops = jnp.sum(weights, axis=1) + counts[:, sites, None, None] * jnp.eye(bond, dtype=jnp.float32)
    right_ops = right_ops.astype(jnp.bfloat16)
    left_ops = operators[0, 0].reshape(sites, cols, firsts, cols, firsts)
    left_ops = jnp.take(jnp.take(left_ops, col_order, axis=1), col_order, axis=3)
    left_ops = left_ops.reshape(sites, bond, bond)

    entering = []
    for chunk in range(chunks):
        pieces = []
        for offset in range(cols):
            start = (col ^ offset) * mine + chunk * step
            piece = lax.dynamic_slice_in_dim(child, start, step, axis=0)
            pieces.append(swap(piece, "col", cols, offset))
        entering.append(pieces)

    flat_child = []
    for offset in range(rows):
        part = lax.dynamic_slice_in_dim(child, (row ^ offset) * share, share, axis=1)
        flat_child.append(swap(part.reshape(tops, share * bond), "row", rows, offset))
    flat_child = jnp.concatenate(flat_child, axis=0)

    columns = []
    for chunk in range(chunks):
        summed = apply_terms(flags, entering[chunk], left_ops, right_ops)
        summed = [swap(summed[offset], "col", cols, offset) for offset in range(cols)]
        for offset in range(rows):
            start = (row ^ offset) * share
            part = jnp.concatenate(
                [lax.dynamic_slice_in_dim(piece, start, share, axis=1) for piece in summed], axis=0
            )
            part = swap(part.reshape(cols * step, share * bond), "row", rows, offset)
            columns.append(
                lax.dot_general(
                    flat_child, part, (((1,), (1,)), ((), ())), preferred_element_type=jnp.float32
                )
            )
    partial = jnp.concatenate(columns, axis=1).reshape(rows, tops, chunks, rows, cols, step)
    partial = jnp.take(partial, row_order, axis=0)
    partial = jnp.take(partial, row_order, axis=3)
    partial = jnp.take(partial, col_order, axis=4)
    partial = jnp.transpose(partial, (0, 1, 3, 4, 2, 5)).reshape(bond, bond)

    envs = share_environments(halves, rows, cols, partial)
    return apply_to_parent(envs, parent)


def solution(mesh):
    placed = (
        P("half", "row", "col", None),
        P("half", None, None, None, None),
        P("half", None, None),
        P("half", None),
        P(("half", "row", "col"), None, None),
    )
    return jax.shard_map(
        functools.partial(on_device, mesh.shape["half"], mesh.shape["row"], mesh.shape["col"]),
        mesh=mesh,
        in_specs=placed,
        out_specs=P(("half", "row", "col"), None, None),
        check_vma=False,
    )
```

```python
import functools

import jax
import jax.numpy as jnp
from jax import lax
from jax.experimental import pallas as pl
from jax.experimental.pallas import tpu as pltpu
from jax.sharding import PartitionSpec as P


def terms_kernel(pieces, batch, groups, flags_ref, *refs):
    piece_refs = refs[:pieces]
    left_ref, right_ref = refs[pieces], refs[pieces + 1]
    out_refs = refs[pieces + 2 : 2 * pieces + 2]
    acc_ref = refs[-1]
    rows = piece_refs[0].shape[1]
    for item in range(batch):
        acc_ref[...] = jnp.zeros_like(acc_ref)

        @pl.when(flags_ref[groups] > 0)
        def _():
            block = jnp.concatenate([ref[item] for ref in piece_refs], axis=0)
            acc_ref[...] = jnp.dot(block, right_ref[groups], preferred_element_type=jnp.float32)

        for group in range(groups):

            @pl.when(flags_ref[group] > 0)
            def _():
                block = jnp.concatenate([ref[item] for ref in piece_refs], axis=0)
                inner = jnp.dot(block, right_ref[group], preferred_element_type=jnp.float32)
                acc_ref[...] += jnp.dot(
                    left_ref[group], inner.astype(jnp.bfloat16), preferred_element_type=jnp.float32
                )

        for place in range(pieces):
            out_refs[place][item] = acc_ref[place * rows : (place + 1) * rows, :].astype(jnp.bfloat16)


def apply_terms(flags, blocks, left_ops, right_ops):
    pieces = len(blocks)
    count, rows, bond = blocks[0].shape
    groups = left_ops.shape[0]
    batch = 2 if count % 2 == 0 else 1
    piece_spec = pl.BlockSpec((batch, rows, bond), lambda a, f: (a, 0, 0))
    flops = 2 * (2 * groups + 1) * count * bond**3
    moved = 4 * count * bond * bond
    return pl.pallas_call(
        functools.partial(terms_kernel, pieces, batch, groups),
        out_shape=[jax.ShapeDtypeStruct((count, rows, bond), jnp.bfloat16)] * pieces,
        grid_spec=pltpu.PrefetchScalarGridSpec(
            num_scalar_prefetch=1,
            grid=(count // batch,),
            in_specs=[piece_spec] * pieces
            + [
                pl.BlockSpec(left_ops.shape, lambda a, f: (0, 0, 0)),
                pl.BlockSpec(right_ops.shape, lambda a, f: (0, 0, 0)),
            ],
            out_specs=[piece_spec] * pieces,
            scratch_shapes=[pltpu.VMEM((bond, bond), jnp.float32)],
        ),
        compiler_params=pltpu.CompilerParams(dimension_semantics=("arbitrary",)),
        cost_estimate=pl.CostEstimate(flops=flops, bytes_accessed=moved, transcendentals=0),
        name="apply_terms",
    )(flags, *blocks, left_ops, right_ops)


MESH_ID = pl.DeviceIdType.MESH


def share_kernel(halves, rows, cols, parts_ref, out_ref, landed, send_sem, recv_sem, line_send, line_recv, plane_send, plane_recv):
    half, row, col = lax.axis_index("half"), lax.axis_index("row"), lax.axis_index("col")

    def place(dh, dr, dc):
        return {
            "half": lax.rem(half + dh, halves),
            "row": lax.rem(row + dr, rows),
            "col": lax.rem(col + dc, cols),
        }

    group = [(dr, dc) for dr in range(rows) for dc in range(cols) if (dr, dc) != (0, 0)]
    plane = [(dh, dc) for dh in range(halves) for dc in range(cols) if (dh, dc) != (0, 0)]
    barrier = pltpu.get_barrier_semaphore()
    greeted = [(0, dr, dc) for dr, dc in group] + [(dh, 0, dc) for dh, dc in plane if dh != 0]
    for spot in greeted:
        pl.semaphore_signal(barrier, inc=1, device_id=place(*spot), device_id_type=MESH_ID)
    pl.semaphore_wait(barrier, len(greeted))

    copies = []
    for dr, dc in group:
        spot = place(0, dr, dc)
        slot = dr * cols + dc
        copy = pltpu.make_async_remote_copy(
            src_ref=parts_ref.at[spot["col"] * rows + spot["row"]],
            dst_ref=landed.at[slot],
            send_sem=send_sem.at[slot],
            recv_sem=recv_sem.at[slot],
            device_id=spot,
            device_id_type=MESH_ID,
        )
        copy.start()
        copies.append(copy)
    total = parts_ref[col * rows + row].astype(jnp.float32)
    for (dr, dc), copy in zip(group, copies):
        copy.wait_recv()
        total = total + landed[dr * cols + dc].astype(jnp.float32)
    mine = (half * cols + col) * rows + row
    out_ref[mine] = total.astype(out_ref.dtype)

    line = []
    for dr in range(1, rows):
        copy = pltpu.make_async_remote_copy(
            src_ref=out_ref.at[mine],
            dst_ref=out_ref.at[mine],
            send_sem=line_send.at[dr],
            recv_sem=line_recv.at[dr],
            device_id=place(0, dr, 0),
            device_id_type=MESH_ID,
        )
        copy.start()
        line.append(copy)
    for copy in line:
        copy.wait_recv()
    block = pl.ds((half * cols + col) * rows, rows)
    for dh, dc in plane:
        slot = dh * cols + dc
        copy = pltpu.make_async_remote_copy(
            src_ref=out_ref.at[block],
            dst_ref=out_ref.at[block],
            send_sem=plane_send.at[slot],
            recv_sem=plane_recv.at[slot],
            device_id=place(dh, 0, dc),
            device_id_type=MESH_ID,
        )
        copy.start()
        copies.append(copy)
    for copy in copies[len(group) :]:
        copy.wait_recv()
    for copy in copies + line:
        copy.wait_send()


def share_environments(halves, rows, cols, partial):
    bond = partial.shape[0]
    slab = bond // (rows * cols)
    dma = pltpu.SemaphoreType.DMA
    return pl.pallas_call(
        functools.partial(share_kernel, halves, rows, cols),
        out_shape=jax.ShapeDtypeStruct((halves * cols * rows, slab, bond), jnp.bfloat16),
        in_specs=[pl.BlockSpec(memory_space=pltpu.VMEM)],
        out_specs=pl.BlockSpec(memory_space=pltpu.VMEM),
        scratch_shapes=[
            pltpu.VMEM((rows * cols, slab, bond), jnp.bfloat16),
            dma((rows * cols,)),
            dma((rows * cols,)),
            dma((rows,)),
            dma((rows,)),
            dma((halves * cols,)),
            dma((halves * cols,)),
        ],
        compiler_params=pltpu.CompilerParams(collective_id=0, has_side_effects=True),
        name="share_environments",
    )(partial.astype(jnp.bfloat16).reshape(rows * cols, slab, bond)).reshape(halves * bond, bond)


def parent_kernel(envs_ref, parent_ref, out_ref):
    bond = parent_ref.shape[1]
    plane = parent_ref[0]
    first = jnp.dot(envs_ref[:bond], plane, preferred_element_type=jnp.float32)
    second = lax.dot_general(
        plane, envs_ref[bond:], (((1,), (1,)), ((), ())), preferred_element_type=jnp.float32
    )
    out_ref[0] = (first + second).astype(out_ref.dtype)


def apply_to_parent(envs, parent):
    count, bond, _ = parent.shape
    spec = pl.BlockSpec((1, bond, bond), lambda c: (c, 0, 0))
    return pl.pallas_call(
        parent_kernel,
        out_shape=jax.ShapeDtypeStruct(parent.shape, parent.dtype),
        grid=(count,),
        in_specs=[pl.BlockSpec(envs.shape, lambda c: (0, 0)), spec],
        out_specs=spec,
        compiler_params=pltpu.CompilerParams(dimension_semantics=("arbitrary",)),
        cost_estimate=pl.CostEstimate(
            flops=4 * count * bond**3, bytes_accessed=4 * count * bond**2, transcendentals=0
        ),
        name="apply_to_parent",
    )(envs, parent)


def meet_kernel(units, slots, *refs):
    held_refs, own_ref, first_refs, second_ref, out_ref = refs[:-5], refs[-5], refs[-4:-2], refs[-2], refs[-1]
    part = pl.program_id(0)
    unit = own_ref.shape[0]

    @pl.when(part == 0)
    def _():
        out_ref[...] = jnp.zeros_like(out_ref)

    begin = 0
    for segment, count in enumerate(units):
        sides = [own_ref] + [ref for ref in ((), first_refs[:1], (first_refs[1], second_ref))[segment]]

        @pl.when((part >= begin) & (part < begin + count))
        def _():
            width = sum(ref.shape[1] for ref in sides)
            entries = [jnp.concatenate([ref[k] for ref in sides], axis=0) for k in range(unit)]
            for (slot, where), ref in zip(slots, held_refs):
                if where not in (None, segment):
                    continue
                total = jnp.zeros((ref.shape[1], width), jnp.float32)
                for k in range(unit):
                    total += lax.dot_general(
                        ref[k], entries[k], (((1,), (1,)), ((), ())), preferred_element_type=jnp.float32
                    )
                out_ref[slot, :, :width] += total

        begin += count


def meet(units, slots, held, own, firsts, second):
    parts = sum(units)
    unit = own.shape[0] // parts
    tops = held[0].shape[1]
    begins = [sum(units[:k]) for k in range(len(units))]

    def spec(value, segment):
        if segment is None:
            return pl.BlockSpec((unit,) + value.shape[1:], lambda g: (g, 0, 0))
        begin, count = begins[segment], units[segment]
        return pl.BlockSpec(
            (unit,) + value.shape[1:], lambda g: (jnp.clip(g - begin, 0, count - 1), 0, 0)
        )

    args = list(held) + [own] + list(firsts) + [second]
    where = [segment for _, segment in slots] + [None, 1, 2, 2]
    out_shape = (1 + max(slot for slot, _ in slots), tops, 3 * own.shape[1])
    return pl.pallas_call(
        functools.partial(meet_kernel, units, slots),
        out_shape=jax.ShapeDtypeStruct(out_shape, jnp.float32),
        grid=(parts,),
        in_specs=[spec(value, segment) for value, segment in zip(args, where)],
        out_specs=pl.BlockSpec(out_shape, lambda g: (0, 0, 0)),
        compiler_params=pltpu.CompilerParams(dimension_semantics=("arbitrary",)),
        cost_estimate=pl.CostEstimate(
            flops=2 * out_shape[0] * tops * own.size, bytes_accessed=2 * sum(v.size for v in args), transcendentals=0
        ),
        name="meet",
    )(*args)


def prepare(cols, operators, term_site, term_leg, firsts, bond):
    col_order = jnp.arange(cols) ^ lax.axis_index("col")
    table = operators[0].astype(jnp.float32)
    site_ids, leg_codes = term_site[0], term_leg[0]
    sites = table.shape[1]
    left_group = jnp.where(leg_codes != 1, site_ids[:, 0], sites)
    right_pick = jnp.where(leg_codes != 0, site_ids[:, 1], sites)
    in_group = (left_group[None, :] == jnp.arange(sites + 1)[:, None]).astype(jnp.float32)
    of_right = (right_pick[:, None] == jnp.arange(sites + 1)[None, :]).astype(jnp.float32)
    counts = jnp.sum(in_group[:, :, None] * of_right[None, :, :], axis=1)
    flags = (jnp.sum(counts, axis=1) > 0).astype(jnp.int32)
    turned = jnp.swapaxes(table[1], 1, 2)
    weights = counts[:, :sites, None, None] * turned[None]
    right_ops = jnp.sum(weights, axis=1) + counts[:, sites, None, None] * jnp.eye(bond, dtype=jnp.float32)
    right_ops = right_ops.astype(jnp.bfloat16)
    left_ops = operators[0, 0].reshape(sites, cols, firsts, cols, firsts)
    left_ops = jnp.take(jnp.take(left_ops, col_order, axis=1), col_order, axis=3)
    return flags, left_ops.reshape(sites, bond, bond), right_ops


def swap(value, axis, size, offset):
    if offset == 0:
        return value
    return lax.ppermute(value, axis, [(k, k ^ offset) for k in range(size)])


def swap_in_rows(value, chosen, cols, offset):
    if offset == 0:
        return value
    pairs = [(r * cols + k, r * cols + (k ^ offset)) for r in chosen for k in range(cols)]
    return lax.ppermute(value, ("row", "col"), pairs)


def four_row_partial(cols, child, flags, left_ops, right_ops):
    tops, firsts, bond = child.shape
    rows = 4
    row = lax.axis_index("row")
    col = lax.axis_index("col")
    mine = tops // cols
    chunks = 4 if mine % 4 == 0 else 1
    step = mine // chunks
    units = (7, 5, 4)
    unit = firsts // sum(units)
    ends = (7 * unit, 12 * unit)

    adjoint_left = jnp.swapaxes(left_ops, 1, 2)
    adjoint_right = jnp.swapaxes(right_ops, 1, 2)
    adjoint_flags = jnp.where(row < 2, flags, 0)

    entering = []
    for chunk in range(chunks):
        pieces = []
        for offset in range(cols):
            start = (col ^ offset) * mine + chunk * step
            piece = lax.dynamic_slice_in_dim(child, start, step, axis=0)
            pieces.append(swap(piece, "col", cols, offset))
        entering.append(pieces)

    turned = jnp.swapaxes(child, 0, 1)
    near, middle, far = turned[: ends[0]], turned[ends[0] : ends[1]], turned[ends[1] :]
    one_near = lax.ppermute(near, "row", [(1, 0), (2, 1), (3, 2)])
    two_near = lax.ppermute(one_near, "row", [(1, 0), (2, 1)])
    one_middle = lax.ppermute(middle, "row", [(2, 1), (3, 2)])
    two_middle = lax.ppermute(one_middle, "row", [(2, 1)])
    one_far = lax.ppermute(far, "row", [(1, 0), (3, 2)])
    back_near = lax.ppermute(jnp.where(row == 2, near, two_near), "row", [(1, 0), (2, 3)])
    back_middle = lax.ppermute(middle, "row", [(2, 3)])
    back_far = lax.ppermute(far, "row", [(2, 3)])
    held = [turned, one_near, one_middle, one_far, two_near, two_middle, back_near, back_middle, back_far]
    slots = [(0, None), (1, 0), (1, 1), (1, 2), (2, 0), (2, 1), (3, 0), (3, 1), (3, 2)]

    met = []
    for chunk in range(chunks):
        straight = apply_terms(flags, entering[chunk], left_ops, right_ops)
        adjoint = apply_terms(adjoint_flags, entering[chunk], adjoint_left, adjoint_right)
        straight = [swap(straight[k], "col", cols, k) for k in range(cols)]
        adjoint = [swap_in_rows(adjoint[k], (0, 1), cols, k) for k in range(cols)]
        own = jnp.concatenate([jnp.swapaxes(piece, 0, 1) for piece in straight + adjoint], axis=1)
        first_middle = lax.ppermute(own[ends[0] : ends[1]], "row", [(0, 1)])
        first_far = lax.ppermute(own[ends[1] :], "row", [(1, 2)])
        second_far = lax.ppermute(own[ends[1] :], "row", [(0, 2)])
        met.append(meet(units, slots, held, own, (first_middle, first_far), second_far))

    col_order = jnp.arange(cols) ^ col
    grid = jnp.stack(met).reshape(chunks, 4, tops, 3, 2, cols, step)
    grid = jnp.take(grid, col_order, axis=5)
    grid = jnp.transpose(grid, (4, 1, 2, 3, 5, 0, 6)).reshape(2, 4, tops, 3, tops)
    grid = grid.at[1, 0, :, 0].set(0.0)
    grid = jnp.where(row == 3, jnp.roll(grid, 1, axis=1), grid)
    grid = jnp.flip(grid, axis=3)
    begin = jnp.where(row == 3, 2, row)
    placed = jnp.zeros((2, 7, tops, 6, tops), jnp.float32)
    placed = lax.dynamic_update_slice(placed, grid, (0, begin, 0, row, 0))[:, :4, :, 2:]
    return placed[0].reshape(bond, bond) + placed[1].reshape(bond, bond).T


def plain_partial(rows, cols, child, flags, left_ops, right_ops):
    tops, firsts, bond = child.shape
    row = lax.axis_index("row")
    col = lax.axis_index("col")
    row_order = jnp.arange(rows) ^ row
    col_order = jnp.arange(cols) ^ col
    mine = tops // cols
    share = firsts // rows
    chunks = 4 if mine % 4 == 0 else 1
    step = mine // chunks

    entering = []
    for chunk in range(chunks):
        pieces = []
        for offset in range(cols):
            start = (col ^ offset) * mine + chunk * step
            piece = lax.dynamic_slice_in_dim(child, start, step, axis=0)
            pieces.append(swap(piece, "col", cols, offset))
        entering.append(pieces)

    flat_child = []
    for offset in range(rows):
        part = lax.dynamic_slice_in_dim(child, (row ^ offset) * share, share, axis=1)
        flat_child.append(swap(part.reshape(tops, share * bond), "row", rows, offset))
    flat_child = jnp.concatenate(flat_child, axis=0)

    columns = []
    for chunk in range(chunks):
        summed = apply_terms(flags, entering[chunk], left_ops, right_ops)
        summed = [swap(summed[offset], "col", cols, offset) for offset in range(cols)]
        for offset in range(rows):
            start = (row ^ offset) * share
            part = jnp.concatenate(
                [lax.dynamic_slice_in_dim(piece, start, share, axis=1) for piece in summed], axis=0
            )
            part = swap(part.reshape(cols * step, share * bond), "row", rows, offset)
            columns.append(
                lax.dot_general(
                    flat_child, part, (((1,), (1,)), ((), ())), preferred_element_type=jnp.float32
                )
            )
    partial = jnp.concatenate(columns, axis=1).reshape(rows, tops, chunks, rows, cols, step)
    partial = jnp.take(partial, row_order, axis=0)
    partial = jnp.take(partial, row_order, axis=3)
    partial = jnp.take(partial, col_order, axis=4)
    return jnp.transpose(partial, (0, 1, 3, 4, 2, 5)).reshape(bond, bond)


def on_device(halves, rows, cols, children, operators, term_site, term_leg, parent):
    child = children[0]
    flags, left_ops, right_ops = prepare(cols, operators, term_site, term_leg, child.shape[1], child.shape[2])
    if rows == 4:
        partial = four_row_partial(cols, child, flags, left_ops, right_ops)
    else:
        partial = plain_partial(rows, cols, child, flags, left_ops, right_ops)
    envs = share_environments(halves, rows, cols, partial)
    return apply_to_parent(envs, parent)


def solution(mesh):
    placed = (
        P("half", "row", "col", None),
        P("half", None, None, None, None),
        P("half", None, None),
        P("half", None),
        P(("half", "row", "col"), None, None),
    )
    return jax.shard_map(
        functools.partial(on_device, mesh.shape["half"], mesh.shape["row"], mesh.shape["col"]),
        mesh=mesh,
        in_specs=placed,
        out_specs=P(("half", "row", "col"), None, None),
        check_vma=False,
    )
```

```python
import functools

import jax
import jax.numpy as jnp
from jax import lax
from jax.experimental import pallas as pl
from jax.experimental.pallas import tpu as pltpu
from jax.sharding import PartitionSpec as P


def terms_kernel(pieces, batch, groups, flags_ref, *refs):
    piece_refs = refs[:pieces]
    left_ref, right_ref = refs[pieces], refs[pieces + 1]
    out_refs = refs[pieces + 2 : 2 * pieces + 2]
    acc_ref = refs[-1]
    rows = piece_refs[0].shape[1]
    for item in range(batch):
        acc_ref[...] = jnp.zeros_like(acc_ref)

        @pl.when(flags_ref[groups] > 0)
        def _():
            block = jnp.concatenate([ref[item] for ref in piece_refs], axis=0)
            acc_ref[...] = jnp.dot(block, right_ref[groups], preferred_element_type=jnp.float32)

        for group in range(groups):

            @pl.when(flags_ref[group] > 0)
            def _():
                block = jnp.concatenate([ref[item] for ref in piece_refs], axis=0)
                inner = jnp.dot(block, right_ref[group], preferred_element_type=jnp.float32)
                acc_ref[...] += jnp.dot(
                    left_ref[group], inner.astype(jnp.bfloat16), preferred_element_type=jnp.float32
                )

        for place in range(pieces):
            out_refs[place][item] = acc_ref[place * rows : (place + 1) * rows, :].astype(jnp.bfloat16)


def apply_terms(flags, blocks, left_ops, right_ops):
    pieces = len(blocks)
    count, rows, bond = blocks[0].shape
    groups = left_ops.shape[0]
    batch = 2 if count % 2 == 0 else 1
    piece_spec = pl.BlockSpec((batch, rows, bond), lambda a, f: (a, 0, 0))
    flops = 2 * (2 * groups + 1) * count * bond**3
    moved = 4 * count * bond * bond
    return pl.pallas_call(
        functools.partial(terms_kernel, pieces, batch, groups),
        out_shape=[jax.ShapeDtypeStruct((count, rows, bond), jnp.bfloat16)] * pieces,
        grid_spec=pltpu.PrefetchScalarGridSpec(
            num_scalar_prefetch=1,
            grid=(count // batch,),
            in_specs=[piece_spec] * pieces
            + [
                pl.BlockSpec(left_ops.shape, lambda a, f: (0, 0, 0)),
                pl.BlockSpec(right_ops.shape, lambda a, f: (0, 0, 0)),
            ],
            out_specs=[piece_spec] * pieces,
            scratch_shapes=[pltpu.VMEM((bond, bond), jnp.float32)],
        ),
        compiler_params=pltpu.CompilerParams(dimension_semantics=("arbitrary",)),
        cost_estimate=pl.CostEstimate(flops=flops, bytes_accessed=moved, transcendentals=0),
        name="apply_terms",
    )(flags, *blocks, left_ops, right_ops)


MESH_ID = pl.DeviceIdType.MESH


def share_kernel(halves, rows, cols, parts_ref, out_ref, landed, send_sem, recv_sem, line_send, line_recv, plane_send, plane_recv):
    half, row, col = lax.axis_index("half"), lax.axis_index("row"), lax.axis_index("col")

    def place(dh, dr, dc):
        return {
            "half": lax.rem(half + dh, halves),
            "row": lax.rem(row + dr, rows),
            "col": lax.rem(col + dc, cols),
        }

    group = [(dr, dc) for dr in range(rows) for dc in range(cols) if (dr, dc) != (0, 0)]
    plane = [(dh, dc) for dh in range(halves) for dc in range(cols) if (dh, dc) != (0, 0)]
    barrier = pltpu.get_barrier_semaphore()
    greeted = [(0, dr, dc) for dr, dc in group] + [(dh, 0, dc) for dh, dc in plane if dh != 0]
    for spot in greeted:
        pl.semaphore_signal(barrier, inc=1, device_id=place(*spot), device_id_type=MESH_ID)
    pl.semaphore_wait(barrier, len(greeted))

    copies = []
    for dr, dc in group:
        spot = place(0, dr, dc)
        slot = dr * cols + dc
        copy = pltpu.make_async_remote_copy(
            src_ref=parts_ref.at[spot["col"] * rows + spot["row"]],
            dst_ref=landed.at[slot],
            send_sem=send_sem.at[slot],
            recv_sem=recv_sem.at[slot],
            device_id=spot,
            device_id_type=MESH_ID,
        )
        copy.start()
        copies.append(copy)
    total = parts_ref[col * rows + row].astype(jnp.float32)
    for (dr, dc), copy in zip(group, copies):
        copy.wait_recv()
        total = total + landed[dr * cols + dc].astype(jnp.float32)
    mine = (half * cols + col) * rows + row
    out_ref[mine] = total.astype(out_ref.dtype)

    line = []
    for dr in range(1, rows):
        copy = pltpu.make_async_remote_copy(
            src_ref=out_ref.at[mine],
            dst_ref=out_ref.at[mine],
            send_sem=line_send.at[dr],
            recv_sem=line_recv.at[dr],
            device_id=place(0, dr, 0),
            device_id_type=MESH_ID,
        )
        copy.start()
        line.append(copy)
    for copy in line:
        copy.wait_recv()
    block = pl.ds((half * cols + col) * rows, rows)
    for dh, dc in plane:
        slot = dh * cols + dc
        copy = pltpu.make_async_remote_copy(
            src_ref=out_ref.at[block],
            dst_ref=out_ref.at[block],
            send_sem=plane_send.at[slot],
            recv_sem=plane_recv.at[slot],
            device_id=place(dh, 0, dc),
            device_id_type=MESH_ID,
        )
        copy.start()
        copies.append(copy)
    for copy in copies[len(group) :]:
        copy.wait_recv()
    for copy in copies + line:
        copy.wait_send()


def share_environments(halves, rows, cols, partial):
    bond = partial.shape[0]
    slab = bond // (rows * cols)
    dma = pltpu.SemaphoreType.DMA
    return pl.pallas_call(
        functools.partial(share_kernel, halves, rows, cols),
        out_shape=jax.ShapeDtypeStruct((halves * cols * rows, slab, bond), jnp.bfloat16),
        in_specs=[pl.BlockSpec(memory_space=pltpu.VMEM)],
        out_specs=pl.BlockSpec(memory_space=pltpu.VMEM),
        scratch_shapes=[
            pltpu.VMEM((rows * cols, slab, bond), jnp.bfloat16),
            dma((rows * cols,)),
            dma((rows * cols,)),
            dma((rows,)),
            dma((rows,)),
            dma((halves * cols,)),
            dma((halves * cols,)),
        ],
        compiler_params=pltpu.CompilerParams(collective_id=0, has_side_effects=True),
        name="share_environments",
    )(partial.astype(jnp.bfloat16).reshape(rows * cols, slab, bond)).reshape(halves * bond, bond)


def parent_kernel(envs_ref, parent_ref, out_ref):
    bond = parent_ref.shape[1]
    plane = parent_ref[0]
    first = jnp.dot(envs_ref[:bond], plane, preferred_element_type=jnp.float32)
    second = lax.dot_general(
        plane, envs_ref[bond:], (((1,), (1,)), ((), ())), preferred_element_type=jnp.float32
    )
    out_ref[0] = (first + second).astype(out_ref.dtype)


def apply_to_parent(envs, parent):
    count, bond, _ = parent.shape
    spec = pl.BlockSpec((1, bond, bond), lambda c: (c, 0, 0))
    return pl.pallas_call(
        parent_kernel,
        out_shape=jax.ShapeDtypeStruct(parent.shape, parent.dtype),
        grid=(count,),
        in_specs=[pl.BlockSpec(envs.shape, lambda c: (0, 0)), spec],
        out_specs=spec,
        compiler_params=pltpu.CompilerParams(dimension_semantics=("arbitrary",)),
        cost_estimate=pl.CostEstimate(
            flops=4 * count * bond**3, bytes_accessed=4 * count * bond**2, transcendentals=0
        ),
        name="apply_to_parent",
    )(envs, parent)


def meet_kernel(units, row_ref, held_ref, one_ref, two_ref, back_ref, own_ref, middle_ref, far_ref, second_ref, out_ref):
    part = pl.program_id(0)
    unit, width = own_ref.shape[:2]
    row = row_ref[0]
    ends = (units[0], units[0] + units[1], sum(units))
    segments = (part < ends[0], (part >= ends[0]) & (part < ends[1]), part >= ends[1])

    @pl.when(part == 0)
    def _():
        out_ref[...] = jnp.zeros_like(out_ref)

    holders = (
        (held_ref, ((0, 1, 2, 3),) * 3),
        (one_ref, ((0, 1, 2), (1, 2), (0, 2))),
        (two_ref, ((0, 1), (1,), ())),
        (back_ref, ((0, 3), (3,), (3,))),
    )
    sides = (
        (own_ref, 0, ((0, 1, 2, 3),) * 3),
        (middle_ref, 1, ((), (1,), ())),
        (far_ref, 1, ((), (), (2,))),
        (second_ref, 2, ((), (), (2,))),
    )
    for segment in range(3):
        for slot, (ref, rows_held) in enumerate(holders):
            for side_ref, side, rows_side in sides:
                rows_both = sorted(set(rows_held[segment]) & set(rows_side[segment]))
                if not rows_both:
                    continue
                fits = functools.reduce(jnp.logical_or, [row == r for r in rows_both])

                @pl.when(segments[segment] & fits)
                def _():
                    total = jnp.zeros((ref.shape[1], width), jnp.float32)
                    for k in range(unit):
                        total += lax.dot_general(
                            ref[k], side_ref[k], (((1,), (1,)), ((), ())), preferred_element_type=jnp.float32
                        )
                    out_ref[slot, :, side * width : (side + 1) * width] += total


def meet(units, row, held, one, two, back, own, middle, far, second):
    parts = sum(units)
    unit = own.shape[0] // parts
    tops, width = held.shape[1], own.shape[1]
    ends = (units[0], units[0] + units[1])

    def spec(value, begin, count, rows_used):
        def index(g, r):
            used = functools.reduce(jnp.logical_or, [r[0] == k for k in rows_used])
            return (jnp.where(used, jnp.clip(g - begin, 0, count - 1), 0), 0, 0)

        return pl.BlockSpec((unit,) + value.shape[1:], index)

    args = (held, one, two, back, own, middle, far, second)
    specs = [
        spec(held, 0, parts, (0, 1, 2, 3)),
        spec(one, 0, parts, (0, 1, 2)),
        spec(two, 0, ends[1], (0, 1)),
        spec(back, 0, parts, (0, 3)),
        spec(own, 0, parts, (0, 1, 2, 3)),
        spec(middle, ends[0], units[1], (1,)),
        spec(far, ends[1], units[2], (2,)),
        spec(second, ends[1], units[2], (2,)),
    ]
    out_shape = (4, tops, 3 * width)
    return pl.pallas_call(
        functools.partial(meet_kernel, units),
        out_shape=jax.ShapeDtypeStruct(out_shape, jnp.float32),
        grid_spec=pltpu.PrefetchScalarGridSpec(
            num_scalar_prefetch=1,
            grid=(parts,),
            in_specs=specs,
            out_specs=pl.BlockSpec(out_shape, lambda g, r: (0, 0, 0)),
        ),
        compiler_params=pltpu.CompilerParams(dimension_semantics=("arbitrary",)),
        name="meet",
    )(row[None], *args)


def sweep_kernel(
    cols, chunks, units, child, turned, lefts, rights,
    own, middle, far, second, one, two, back, staged,
    entered, total, packed, local_sem, enter_send, enter_recv, turn_send, turn_recv, held_send, held_recv, sums_send, sums_recv,
):
    half, row, col = lax.axis_index("half"), lax.axis_index("row"), lax.axis_index("col")
    tops, firsts, bond = child.shape
    mine = tops // cols
    step = mine // chunks
    groups = lefts.shape[1]
    unit = firsts // sum(units)
    ends = (units[0] * unit, (units[0] + units[1]) * unit)
    near_part, middle_part = pl.ds(0, ends[0]), pl.ds(ends[0], ends[1] - ends[0])
    far_part = pl.ds(ends[1], firsts - ends[1])
    left_row, right_row, far_row = lax.rem(row + 3, 4), lax.rem(row + 1, 4), lax.rem(row + 2, 4)
    kinds = jnp.where(row < 2, 2, 1)

    def remote(src, dst, send, recv, to_row, to_col):
        return pltpu.make_async_remote_copy(
            src_ref=src,
            dst_ref=dst,
            send_sem=send,
            recv_sem=recv,
            device_id={"half": half, "row": to_row, "col": to_col},
            device_id_type=MESH_ID,
        )

    def enter(q, o):
        to = lax.rem(col + o, cols)
        return remote(
            child.at[pl.ds(to * mine + q * step, step)],
            entered.at[q, :, pl.ds(pl.multiple_of(col * firsts, firsts), firsts)],
            enter_send.at[q, o],
            enter_recv.at[q, o],
            row,
            to,
        )

    def enter_own(q):
        return pltpu.make_async_copy(
            child.at[pl.ds(col * mine + q * step, step)],
            entered.at[q, :, pl.ds(pl.multiple_of(col * firsts, firsts), firsts)],
            local_sem.at[0],
        )

    def give(q, t, o):
        to = lax.rem(col + o, cols)
        return remote(
            staged.at[q, t, pl.ds(to * firsts, firsts)],
            own.at[:, q, t, col],
            turn_send.at[q, t, o],
            turn_recv.at[q, t, o],
            row,
            to,
        )

    blocks = (
        (turned.at[near_part], one.at[near_part], left_row),
        (turned.at[middle_part], one.at[middle_part], left_row),
        (turned.at[far_part], one.at[far_part], left_row),
        (one.at[near_part], two.at[near_part], left_row),
        (one.at[middle_part], two.at[middle_part], left_row),
        (two.at[near_part], back.at[near_part], left_row),
        (turned, back, right_row),
    )

    def block(n):
        src, dst, to = blocks[n]
        return remote(src, dst, held_send.at[n], held_recv.at[n], to, col)

    def sums(n, q, t):
        src, dst, to = (
            (own.at[middle_part, q, t], middle.at[:, q, t], right_row),
            (own.at[far_part, q, t], far.at[:, q, t], right_row),
            (own.at[far_part, q, t], second.at[:, q, t], far_row),
        )[n]
        return remote(src, dst, sums_send.at[n, q, t], sums_recv.at[n, q, t], to, col)

    def terms(q, t):
        def one_top(a, carry):
            total[a] = jnp.dot(entered[q, a], rights[t, groups], preferred_element_type=jnp.float32)
            for g in range(groups):
                inner = jnp.dot(entered[q, a], rights[t, g], preferred_element_type=jnp.float32)
                total[a] += jnp.dot(lefts[t, g], inner.astype(jnp.bfloat16), preferred_element_type=jnp.float32)
            return carry

        lax.fori_loop(0, step, one_top, 0)

        def turn(n, carry):
            rows = pl.ds(pl.multiple_of(n * 32, 32), 32)
            packed[rows] = jnp.swapaxes(total[:, rows, :], 0, 1).astype(jnp.bfloat16)
            return carry

        lax.fori_loop(0, cols * firsts // 32, turn, 0)
        out = pltpu.make_async_copy(packed, staged.at[q, t], local_sem.at[0])
        keep = pltpu.make_async_copy(
            packed.at[pl.ds(pl.multiple_of(col * firsts, firsts), firsts)], own.at[:, q, t, col], local_sem.at[1]
        )
        out.start()
        keep.start()
        out.wait()
        keep.wait()
        for o in range(1, cols):
            give(q, t, o).start()

    def pass_on(q):
        def kind(t, carry):
            for o in range(1, cols):
                give(q, t, o).wait_recv()

            @pl.when(row == 0)
            def _():
                sums(0, q, t).start()
                sums(2, q, t).start()

            @pl.when(row == 1)
            def _():
                sums(1, q, t).start()

            return carry

        lax.fori_loop(0, kinds, kind, 0)

    barrier = pltpu.get_barrier_semaphore()
    for o in range(1, cols):
        pl.semaphore_signal(
            barrier,
            inc=1,
            device_id={"half": half, "row": row, "col": lax.rem(col + o, cols)},
            device_id_type=MESH_ID,
        )
    for to in (left_row, right_row, far_row):
        pl.semaphore_signal(
            barrier, inc=1, device_id={"half": half, "row": to, "col": col}, device_id_type=MESH_ID
        )
    pl.semaphore_wait(barrier, cols + 2)

    for o in range(1, cols):
        enter(0, o).start()

    @pl.when(row > 0)
    def _():
        block(0).start()

    @pl.when(row == 3)
    def _():
        block(1).start()
        block(2).start()

    @pl.when(row == 1)
    def _():
        block(2).start()

    @pl.when(row == 2)
    def _():
        block(6).start()

    for o in range(1, cols):
        enter(1, o).start()

    def chunk(q, carry):
        mine_in = enter_own(q)
        mine_in.start()
        mine_in.wait()
        for o in range(1, cols):
            enter(q, o).wait_recv()

        def kind(t, inner_carry):
            terms(q, t)
            return inner_carry

        lax.fori_loop(0, kinds, kind, 0)

        @pl.when(q + 2 < chunks)
        def _():
            for o in range(1, cols):
                enter(q + 2, o).start()

        @pl.when((q == 1) & (row < 3))
        def _():
            block(0).wait_recv()

            @pl.when(row > 0)
            def _():
                block(3).start()

            @pl.when(row == 2)
            def _():
                block(1).start()

        @pl.when(q > 0)
        def _():
            pass_on(q - 1)

        @pl.when((q == 2) & (row == 1))
        def _():
            block(3).wait_recv()
            block(5).start()

        @pl.when((q == 2) & (row == 2))
        def _():
            block(1).wait_recv()
            block(4).start()

        return carry

    lax.fori_loop(0, chunks, chunk, 0)
    pass_on(chunks - 1)

    received = ((2, 3, 5), (1, 4), (2,), (6,))
    started = ((), (0, 2, 3, 5), (0, 1, 3, 4, 6), (0, 1, 2))
    for r in range(4):

        @pl.when(row == r)
        def _():
            for n in received[r]:
                block(n).wait_recv()
            for n in started[r]:
                block(n).wait_send()

    def settle(q, carry):
        for o in range(1, cols):
            enter(q, o).wait_send()

        def kind(t, inner_carry):
            for o in range(1, cols):
                give(q, t, o).wait_send()
            return inner_carry

        lax.fori_loop(0, kinds, kind, 0)
        for t in range(2):

            @pl.when(row == 0)
            def _():
                sums(0, q, t).wait_send()
                sums(2, q, t).wait_send()

            @pl.when(row == 1)
            def _():
                sums(1, q, t).wait_send()
                sums(0, q, t).wait_recv()

            @pl.when(row == 2)
            def _():
                sums(1, q, t).wait_recv()
                sums(2, q, t).wait_recv()

        return carry

    lax.fori_loop(0, chunks, settle, 0)


def sweep(cols, chunks, units, child, turned, lefts, rights):
    tops, firsts, bond = child.shape
    step = tops // cols // chunks
    unit = firsts // sum(units)
    lengths = (firsts, units[1] * unit, units[2] * unit, units[2] * unit)
    anywhere = pl.BlockSpec(memory_space=pl.ANY)
    dma = pltpu.SemaphoreType.DMA

    def shaped(*dims):
        return jax.ShapeDtypeStruct(dims, jnp.bfloat16)

    out_shape = [shaped(n, chunks, 2, cols, step, bond) for n in lengths]
    out_shape += [
        shaped(firsts, tops, bond),
        shaped((units[0] + units[1]) * unit, tops, bond),
        shaped(firsts, tops, bond),
        shaped(chunks, 2, cols * firsts, step, bond),
    ]
    outs = pl.pallas_call(
        functools.partial(sweep_kernel, cols, chunks, units),
        out_shape=out_shape,
        in_specs=[anywhere, anywhere] + [pl.BlockSpec(memory_space=pltpu.VMEM)] * 2,
        out_specs=[anywhere] * len(out_shape),
        scratch_shapes=[
            pltpu.VMEM((chunks, step, cols * firsts, bond), jnp.bfloat16),
            pltpu.VMEM((step, cols * firsts, bond), jnp.float32),
            pltpu.VMEM((cols * firsts, step, bond), jnp.bfloat16),
            dma((2,)),
            dma((chunks, cols)),
            dma((chunks, cols)),
            dma((chunks, 2, cols)),
            dma((chunks, 2, cols)),
            dma((7,)),
            dma((7,)),
            dma((3, chunks, 2)),
            dma((3, chunks, 2)),
        ],
        compiler_params=pltpu.CompilerParams(collective_id=1, has_side_effects=True),
        name="sweep",
    )(child, turned, lefts, rights)
    return [out.reshape(out.shape[0], 2 * chunks * cols * step, bond) for out in outs[:4]] + list(outs[4:7])


def term_counts(operators, term_site, term_leg):
    site_ids, leg_codes = term_site[0], term_leg[0]
    sites = operators.shape[2]
    left_group = jnp.where(leg_codes != 1, site_ids[:, 0], sites)
    right_pick = jnp.where(leg_codes != 0, site_ids[:, 1], sites)
    in_group = (left_group[None, :] == jnp.arange(sites + 1)[:, None]).astype(jnp.float32)
    of_right = (right_pick[:, None] == jnp.arange(sites + 1)[None, :]).astype(jnp.float32)
    return jnp.sum(in_group[:, :, None] * of_right[None, :, :], axis=1), sites


def prepare(cols, operators, term_site, term_leg, firsts, bond):
    col_order = jnp.arange(cols) ^ lax.axis_index("col")
    table = operators[0].astype(jnp.float32)
    counts, sites = term_counts(operators, term_site, term_leg)
    flags = (jnp.sum(counts, axis=1) > 0).astype(jnp.int32)
    turned = jnp.swapaxes(table[1], 1, 2)
    weights = counts[:, :sites, None, None] * turned[None]
    right_ops = jnp.sum(weights, axis=1) + counts[:, sites, None, None] * jnp.eye(bond, dtype=jnp.float32)
    right_ops = right_ops.astype(jnp.bfloat16)
    left_ops = operators[0, 0].reshape(sites, cols, firsts, cols, firsts)
    left_ops = jnp.take(jnp.take(left_ops, col_order, axis=1), col_order, axis=3)
    return flags, left_ops.reshape(sites, bond, bond), right_ops


def swap(value, axis, size, offset):
    if offset == 0:
        return value
    return lax.ppermute(value, axis, [(k, k ^ offset) for k in range(size)])


def four_row_partial(cols, child, operators, term_site, term_leg):
    tops, firsts, bond = child.shape
    row = lax.axis_index("row")
    chunks, units = 4, (7, 5, 4)
    step = tops // cols // chunks
    counts, sites = term_counts(operators, term_site, term_leg)
    table = operators[0, 1].astype(jnp.float32)
    rights = jnp.sum(counts[:, :sites, None, None] * table[None], axis=1)
    rights = (rights + counts[:, sites, None, None] * jnp.eye(bond, dtype=jnp.float32)).astype(jnp.bfloat16)
    rights = jnp.stack([jnp.swapaxes(rights, 1, 2), rights])
    lefts = jnp.stack([operators[0, 0], jnp.swapaxes(operators[0, 0], 1, 2)])
    turned = jnp.swapaxes(child, 0, 1)
    own, middle, far, second, one, two, back = sweep(cols, chunks, units, child, turned, lefts, rights)
    grid = meet(units, row, turned, one, two, back, own, middle, far, second)

    grid = grid.reshape(4, tops, 3, chunks, 2, cols, step)
    grid = jnp.transpose(grid, (4, 0, 1, 2, 5, 3, 6)).reshape(2, 4, tops, 3, tops)
    grid = grid.at[1, 0, :, 0].set(0.0)
    grid = jnp.where(row < 2, grid, grid.at[1, :, :, 0].set(0.0))
    grid = jnp.where(row == 3, jnp.roll(grid, 1, axis=1), grid)
    grid = jnp.flip(grid, axis=3)
    begin = jnp.where(row == 3, 2, row)
    placed = jnp.zeros((2, 7, tops, 6, tops), jnp.float32)
    placed = lax.dynamic_update_slice(placed, grid, (0, begin, 0, row, 0))[:, :4, :, 2:]
    return placed[0].reshape(bond, bond) + placed[1].reshape(bond, bond).T


def plain_partial(rows, cols, child, flags, left_ops, right_ops):
    tops, firsts, bond = child.shape
    row = lax.axis_index("row")
    col = lax.axis_index("col")
    row_order = jnp.arange(rows) ^ row
    col_order = jnp.arange(cols) ^ col
    mine = tops // cols
    share = firsts // rows
    chunks = 4 if mine % 4 == 0 else 1
    step = mine // chunks

    entering = []
    for chunk in range(chunks):
        pieces = []
        for offset in range(cols):
            start = (col ^ offset) * mine + chunk * step
            piece = lax.dynamic_slice_in_dim(child, start, step, axis=0)
            pieces.append(swap(piece, "col", cols, offset))
        entering.append(pieces)

    flat_child = []
    for offset in range(rows):
        part = lax.dynamic_slice_in_dim(child, (row ^ offset) * share, share, axis=1)
        flat_child.append(swap(part.reshape(tops, share * bond), "row", rows, offset))
    flat_child = jnp.concatenate(flat_child, axis=0)

    columns = []
    for chunk in range(chunks):
        summed = apply_terms(flags, entering[chunk], left_ops, right_ops)
        summed = [swap(summed[offset], "col", cols, offset) for offset in range(cols)]
        for offset in range(rows):
            start = (row ^ offset) * share
            part = jnp.concatenate(
                [lax.dynamic_slice_in_dim(piece, start, share, axis=1) for piece in summed], axis=0
            )
            part = swap(part.reshape(cols * step, share * bond), "row", rows, offset)
            columns.append(
                lax.dot_general(
                    flat_child, part, (((1,), (1,)), ((), ())), preferred_element_type=jnp.float32
                )
            )
    partial = jnp.concatenate(columns, axis=1).reshape(rows, tops, chunks, rows, cols, step)
    partial = jnp.take(partial, row_order, axis=0)
    partial = jnp.take(partial, row_order, axis=3)
    partial = jnp.take(partial, col_order, axis=4)
    return jnp.transpose(partial, (0, 1, 3, 4, 2, 5)).reshape(bond, bond)


def on_device(halves, rows, cols, children, operators, term_site, term_leg, parent):
    child = children[0]
    tops, firsts, bond = child.shape
    if rows == 4 and tops % (32 * cols) == 0 and firsts % 128 == 0:
        partial = four_row_partial(cols, child, operators, term_site, term_leg)
    else:
        flags, left_ops, right_ops = prepare(cols, operators, term_site, term_leg, firsts, bond)
        partial = plain_partial(rows, cols, child, flags, left_ops, right_ops)
    envs = share_environments(halves, rows, cols, partial)
    return apply_to_parent(envs, parent)


def solution(mesh):
    placed = (
        P("half", "row", "col", None),
        P("half", None, None, None, None),
        P("half", None, None),
        P("half", None),
        P(("half", "row", "col"), None, None),
    )
    return jax.shard_map(
        functools.partial(on_device, mesh.shape["half"], mesh.shape["row"], mesh.shape["col"]),
        mesh=mesh,
        in_specs=placed,
        out_specs=P(("half", "row", "col"), None, None),
        check_vma=False,
    )
```
